32 devices in a mesh: occ: 8 (over z, y), vir: 4 (over x, core).
Axes of the slice: x: 2, y: 2, z: 4, core: 2. Of those that a mesh axis runs over, the one named last changes fastest.
Arguments:
- w_cycle: bfloat16 [512, 64, 64, 512], P(None, 'occ', None, 'vir'), may hold values from -0.03125 to 0.03125
- q_cur: float32 [512, 64, 768], P('vir', 'occ'), may hold values from -6 to 6
- q_prev: float32 [512, 64, 768], P('vir', 'occ'), may hold values from -6 to 6
- b_prev: float32 [16, 16], replicated, may hold values from -5 to 5
- e_vir: float32 [512], P('vir'), may hold values from 0.5 to 4
- e_occ: float32 [64], replicated, may hold values from -2 to -0.3
Outputs:
- q_next: float32 [512, 64, 768], P('vir', 'occ')
- alpha_block: float32 [16, 16], replicated
- b_next: float32 [16, 16], replicated
The draws below stay inside these ranges and needn't reach their ends.
All inputs are finite; a program needn't handle non-finite values.
Results may differ from the reference program's by a relative error of at most 0.0012.
Values may be sent and summed in bfloat16 or wider, within the bound.
No kernel may reach another device: no remote copies, remote signals or barrier semaphores. Data moves between devices by JAX's collectives and lax.ppermute only.
A program may use at most 192 MiB of HBM per device.

```python
import jax
import jax.numpy as jnp
from jax import lax

VS = 512
O = 64
NB = 16
J = 48


def level_of(own_key, dims, split, least, high):
    gain, own = 1.0, jax.random.fold_in(own_key, 6)
    for position, shards_of in split:
        draws = jnp.exp(jax.random.uniform(jax.random.fold_in(own, position), (shards_of,), jnp.float32, least / len(split), high / len(split)))
        gain = gain * jnp.repeat(draws, dims[position] // shards_of).reshape([-1 if axis == position else 1 for axis in range(len(dims))])
    return gain


def gaussian(rng, shape, width, limit, shards=(), kind=jnp.bfloat16):
    drawn = jax.random.normal(rng, shape, jnp.float32) * width
    if len(shards) > 0:
        drawn = level_of(rng, shape, shards, -0.22, 0.18) * drawn
    return jnp.clip(drawn, min=-limit, max=limit).astype(kind)


def setup_inputs(seed: int = 0) -> dict:
    arg_keys = jax.random.split(jax.random.key(seed), 7)
    w_cycle = gaussian(arg_keys[0], (VS, O, O, VS), (O * VS) ** -0.5, 0.03125, ((1, 8), (3, 4)))
    q_cur = gaussian(arg_keys[1], (VS, O, J * NB), 1.0, 6.0, ((0, 4), (1, 8)), jnp.float32)
    q_prev = gaussian(arg_keys[2], (VS, O, J * NB), 1.0, 6.0, ((0, 4), (1, 8)), jnp.float32)
    b_prev = gaussian(arg_keys[3], (NB, NB), 1.0, 5.0, (), jnp.float32)
    e_vir = jnp.clip(0.5 + 3.5 * jax.random.uniform(arg_keys[4], (VS,), jnp.float32) ** level_of(arg_keys[4], (VS,), ((0, 4),), -0.2, 0.2), 0.5, 4.0)
    e_occ = jnp.clip(jax.random.uniform(arg_keys[5], (O,), jnp.float32, -2.0, -0.3), -2.0, -0.3)
    return {"w_cycle": w_cycle, "q_cur": q_cur, "q_prev": q_prev, "b_prev": b_prev, "e_vir": e_vir, "e_occ": e_occ}


def inner_block(left_block, right_block):
    return jnp.einsum('aijn,aijm->nm', left_block, right_block, precision=lax.Precision.HIGHEST) / (VS * O * J)

def reference(w_cycle, q_cur, q_prev, b_prev, e_vir, e_occ):
    q_half = q_cur.astype(jnp.bfloat16)
    w_flat = w_cycle.reshape(VS * O, O * VS)
    q_flat = jnp.transpose(q_half, (1, 0, 2)).reshape(O * VS, J * NB)
    cycle_term = jnp.dot(w_flat.astype(jnp.float32), q_flat.astype(jnp.float32), preferred_element_type=jnp.float32).reshape(VS, O, J, NB)
    energy_gap = e_vir[:, None, None] - e_occ[None, :, None] - e_occ[None, None, :J]
    cur_four = q_cur.reshape(VS, O, J, NB)
    prev_four = q_prev.reshape(VS, O, J, NB)
    sigma_block = cycle_term + energy_gap[:, :, :, None] * cur_four
    alpha_block = inner_block(cur_four, sigma_block)
    upper_t = jnp.triu(b_prev).T
    residual = sigma_block - jnp.einsum('aijn,nm->aijm', cur_four, alpha_block, precision=lax.Precision.HIGHEST)
    residual = residual - jnp.einsum('aijn,nm->aijm', prev_four, upper_t, precision=lax.Precision.HIGHEST)
    gram_block = inner_block(residual, residual)
    lower_factor = jnp.linalg.cholesky(gram_block)
    b_next = lower_factor.T
    inv_upper = jax.scipy.linalg.solve_triangular(lower_factor, jnp.eye(NB, dtype=jnp.float32), lower=True).T
    q_next = jnp.einsum('aijn,nm->aijm', residual, inv_upper, precision=lax.Precision.HIGHEST)
    return (q_next.reshape(VS, O, J * NB), alpha_block, b_next)
```

```python
import functools

import jax
import jax.numpy as jnp
from jax import lax
from jax.experimental import pallas as pl
from jax.experimental.pallas import tpu as pltpu
from jax.sharding import PartitionSpec as P


BF = jnp.bfloat16
F32 = jnp.float32
HIGH = lax.Precision.HIGHEST
WIDE = 256
LANES = 128
MIB = 1 << 20


def dot(left, right, dims=((1,), (0,)), precision=None):
    return lax.dot_general(left, right, (dims, ((), ())), precision=precision, preferred_element_type=F32)


def halves(value):
    high = value.astype(BF)
    return high, (value - high.astype(F32)).astype(BF)


def dot3(left, right, dims):
    (lh, ll), (rh, rl) = left, right
    return dot(lh, rh, dims) + dot(lh, rl, dims) + dot(ll, rh, dims)


def cycle_first(add, pos, w0, w1, q0, q1, *rest):
    acc = rest[0] if add else None
    out, turned = rest[-2:]
    rows = w0.shape[0] * w0.shape[1]
    depth = w0.shape[2]
    total = acc[...] if add else None
    for place, (w, q) in enumerate(((w0, q0), (w1, q1))):
        by_k = jnp.swapaxes(w[...].astype(F32), 1, 2)
        parts = [by_k[:, k].reshape(rows, w.shape[3]).astype(BF) for k in range(depth)]
        for k in range(depth):
            turned[place * depth + k] = parts[k]
        term = dot(jnp.concatenate(parts, axis=1), q[...].reshape(depth * q.shape[1], q.shape[2]))
        total = term if total is None else total + term
    out[...] = total


def cycle_later(add, turned, q0, q1, *rest):
    acc = rest[0] if add else None
    out = rest[-1]
    depth = q0.shape[0]
    total = acc[...] if add else None
    for place, q in enumerate((q0, q1)):
        lhs = jnp.concatenate([turned[place * depth + k] for k in range(depth)], axis=1)
        term = dot(lhs, q[...].reshape(depth * q.shape[1], q.shape[2]))
        total = term if total is None else total + term
    out[...] = total


def call_first(w, q0, q1, acc, pos, v_loc, tile):
    _, o_loc, _, b_loc = w.shape
    depth, _, cols = q0.shape
    per = v_loc // tile
    steps = 2 * per
    rows = tile * o_loc
    full = 2 * v_loc * o_loc
    wspec = lambda s: pl.BlockSpec(
        (tile, o_loc, depth, b_loc), lambda g, p: (p[g // per] * per + g % per, 0, p[2 + s], 0)
    )
    qspec = pl.BlockSpec((depth, b_loc, cols), lambda g, p: (0, 0, 0))
    aspec = pl.BlockSpec((rows, cols), lambda g, p: (g, 0))
    add = acc is not None
    return pl.pallas_call(
        functools.partial(cycle_first, add),
        grid_spec=pltpu.PrefetchScalarGridSpec(
            num_scalar_prefetch=1,
            grid=(steps,),
            in_specs=[wspec(0), wspec(1), qspec, qspec] + ([aspec] if add else []),
            out_specs=[aspec, pl.BlockSpec((2 * depth, rows, b_loc), lambda g, p: (0, g, 0))],
        ),
        out_shape=[
            jax.ShapeDtypeStruct((full, cols), F32),
            jax.ShapeDtypeStruct((2 * depth, full, b_loc), BF),
        ],
        input_output_aliases={5: 0} if add else {},
        compiler_params=pltpu.CompilerParams(vmem_limit_bytes=44 * MIB),
        cost_estimate=pl.CostEstimate(
            flops=4 * full * depth * b_loc * cols, bytes_accessed=full * (8 * depth * b_loc + 8 * cols), transcendentals=0
        ),
        name="cycle_first",
    )(pos, w, w, q0, q1, *([acc] if add else []))


def call_later(turned, q0, q1, acc, rows):
    depth, b_loc, cols = q0.shape
    full = turned.shape[1]
    aspec = pl.BlockSpec((rows, cols), lambda g: (g, 0))
    qspec = pl.BlockSpec((depth, b_loc, cols), lambda g: (0, 0, 0))
    add = acc is not None
    return pl.pallas_call(
        functools.partial(cycle_later, add),
        grid=(full // rows,),
        in_specs=[pl.BlockSpec((2 * depth, rows, b_loc), lambda g: (0, g, 0)), qspec, qspec] + ([aspec] if add else []),
        out_specs=aspec,
        out_shape=jax.ShapeDtypeStruct((full, cols), F32),
        input_output_aliases={3: 0} if add else {},
        compiler_params=pltpu.CompilerParams(vmem_limit_bytes=44 * MIB),
        cost_estimate=pl.CostEstimate(
            flops=4 * full * depth * b_loc * cols, bytes_accessed=full * (4 * depth * b_loc + 8 * cols), transcendentals=0
        ),
        name="cycle_later",
    )(turned, q0, q1, *([acc] if add else []))


def fold(block, nblock):
    height, width = block.shape
    row = lax.broadcasted_iota(jnp.int32, (WIDE, width), 0) // nblock
    col = lax.broadcasted_iota(jnp.int32, (WIDE, width), 1) // nblock
    sums = []
    for top in range(0, height, WIDE):
        kept = jnp.where(row == col, block[top : top + WIDE], 0.0)
        sums.append(kept.reshape(WIDE // nblock, nblock, width).sum(0))
    total = jnp.concatenate(sums, axis=0)
    lanes = total[:, :LANES]
    for left in range(LANES, width, LANES):
        lanes = lanes + total[:, left : left + LANES]
    shift = LANES // 2
    while shift >= nblock:
        lanes = lanes + pltpu.roll(lanes, shift, 1)
        shift //= 2
    return lanes


def old_kernel(nblock, cur, prev, out, total):
    step = pl.program_id(0)

    @pl.when(step == 0)
    def _():
        total[...] = jnp.zeros_like(total)

    for left in range(0, cur.shape[1], WIDE):
        both = jnp.concatenate([cur[:, left : left + WIDE], prev[:, left : left + WIDE]], axis=1)
        parts = halves(both)
        total[...] += dot3(parts, parts, ((0,), (0,)))

    @pl.when(step == pl.num_programs(0) - 1)
    def _():
        lane = lax.broadcasted_iota(jnp.int32, (2 * nblock, LANES), 1)
        mine = fold(total[:, :WIDE], nblock)
        other = fold(total[:, WIDE:], nblock)
        value = jnp.where((lane >= nblock) & (lane < 2 * nblock), mine, 0.0)
        value = jnp.where((lane >= 2 * nblock) & (lane < 3 * nblock), other, value)
        out[...] = jnp.concatenate([jnp.zeros((nblock, LANES), F32), value], axis=0)


def call_old(cur, prev, nblock, tile):
    rows, cols = cur.shape
    spec = pl.BlockSpec((tile, cols), lambda g: (g, 0))
    return pl.pallas_call(
        functools.partial(old_kernel, nblock),
        grid=(rows // tile,),
        in_specs=[spec, spec],
        out_specs=pl.BlockSpec((3 * nblock, LANES), lambda g: (0, 0)),
        out_shape=jax.ShapeDtypeStruct((3 * nblock, LANES), F32),
        scratch_shapes=[pltpu.VMEM((2 * WIDE, 2 * WIDE), F32)],
        compiler_params=pltpu.CompilerParams(vmem_limit_bytes=32 * MIB),
        cost_estimate=pl.CostEstimate(flops=12 * rows * cols * 2 * WIDE, bytes_accessed=8 * rows * cols, transcendentals=0),
        name="old_blocks",
    )(cur, prev)


def sigma_kernel(nblock, keep, came, cur, prev, row_gap, col_gap, base, sig, out, total):
    step = pl.program_id(0)

    @pl.when(step == 0)
    def _():
        total[...] = jnp.zeros_like(total)

    for left in range(0, cur.shape[1], WIDE):
        here = slice(left, left + WIDE)
        q = cur[:, here]
        gap = jnp.tile(row_gap[...], (1, WIDE // LANES)) - col_gap[:, here]
        value = keep[:, here] + came[:, here].astype(F32) + gap * q
        sig[:, here] = value
        vh, vl = halves(value)
        ch, cl = halves(q)
        ph, pw = halves(prev[:, here])
        highs = jnp.concatenate([vh, ch, ph], axis=1)
        lows = jnp.concatenate([vl, cl, pw], axis=1)
        total[...] += dot3((highs, lows), (vh, vl), ((0,), (0,)))

    @pl.when(step == pl.num_programs(0) - 1)
    def _():
        lane = lax.broadcasted_iota(jnp.int32, (3 * nblock, LANES), 1)
        out[...] = base[...] + jnp.where(lane < nblock, fold(total[...], nblock), 0.0)


def call_sigma(keep, keep_block, came, cur, prev, row_gap, col_gap, base, nblock, left, tile):
    rows = cur.shape[0]
    cols = came.shape[1]
    per = rows // tile
    spec = pl.BlockSpec((tile, cols), lambda g: (g, 0))
    at = left // cols
    qspec = pl.BlockSpec((tile, cols), lambda g: (g, at))
    whole = pl.BlockSpec((3 * nblock, LANES), lambda g: (0, 0))
    return pl.pallas_call(
        functools.partial(sigma_kernel, nblock),
        grid=(per,),
        in_specs=[
            pl.BlockSpec((tile, cols), lambda g: (keep_block * per + g, 0)),
            spec,
            qspec,
            qspec,
            pl.BlockSpec((tile, LANES), lambda g: (g, 0)),
            pl.BlockSpec((1, cols), lambda g: (0, at)),
            whole,
        ],
        out_specs=[spec, whole],
        out_shape=[jax.ShapeDtypeStruct((rows, cols), F32), jax.ShapeDtypeStruct((3 * nblock, LANES), F32)],
        scratch_shapes=[pltpu.VMEM((3 * WIDE, WIDE), F32)],
        compiler_params=pltpu.CompilerParams(vmem_limit_bytes=32 * MIB),
        cost_estimate=pl.CostEstimate(flops=18 * rows * cols * WIDE, bytes_accessed=18 * rows * cols, transcendentals=0),
        name="sigma",
    )(keep, came, cur, prev, row_gap, col_gap, base)


def last_kernel(nblock, count, n_sig, sums, b_prev, cur, prev, *rest):
    sigs, (q_next, alpha_out, b_next, mat_high, mat_low) = rest[:n_sig], rest[n_sig:]

    @pl.when(pl.program_id(0) == 0)
    def _():
        n = nblock
        k = sums[...] / count
        alpha = k[n : 2 * n, :n]
        row = lax.broadcasted_iota(jnp.int32, (n, n), 0)
        col = lax.broadcasted_iota(jnp.int32, (n, n), 1)
        upper = jnp.where(row <= col, b_prev[...], 0.0)
        upper_t = upper.T
        z = jnp.concatenate([-alpha, -upper_t], axis=0)
        k_rs = k[n : 3 * n, :n]
        k_rr = k[n : 3 * n, n : 3 * n]
        lead = ((0,), (0,))
        v = dot(k_rr, z, precision=HIGH)
        gram = (k[:n, :n] + dot(k_rs, z, lead, HIGH)) + dot(z, k_rs + v, lead, HIGH)
        lane = lax.broadcasted_iota(jnp.int32, (n, LANES), 1)
        line = lax.broadcasted_iota(jnp.int32, (n, LANES), 0)
        aug = jnp.concatenate([gram, jnp.zeros((n, LANES - n), F32)], axis=1)
        aug = aug + jnp.where(lane == line + n, 1.0, 0.0)
        for i in range(n):
            root = jnp.sqrt(aug[i : i + 1, i : i + 1])
            scaled = aug[i : i + 1, :] / root
            factor = aug[:, i : i + 1] / root
            aug = jnp.where(line == i, scaled, jnp.where(line > i, aug - factor * scaled, aug))
        alpha_out[...] = alpha
        b_next[...] = jnp.where(row <= col, aug[:, :n], 0.0)
        low_inv = aug[:, n : 2 * n]
        eye = jnp.where(row == col, 1.0, 0.0)
        mats = dot(jnp.concatenate([eye, z], axis=0), low_inv, ((1,), (1,)), HIGH)
        spread = jnp.where(
            lax.broadcasted_iota(jnp.int32, (n, WIDE), 1) % n == lax.broadcasted_iota(jnp.int32, (n, WIDE), 0), 1.0, 0.0
        )
        wide = dot(mats, spread, precision=HIGH)
        same = (
            lax.broadcasted_iota(jnp.int32, (WIDE, WIDE), 0) // n == lax.broadcasted_iota(jnp.int32, (WIDE, WIDE), 1) // n
        )
        for part in range(3):
            block = jnp.concatenate([wide[part * n : (part + 1) * n]] * (WIDE // n), axis=0)
            high, low = halves(jnp.where(same, block, 0.0))
            mat_high[part * WIDE : (part + 1) * WIDE] = high
            mat_low[part * WIDE : (part + 1) * WIDE] = low

    mats = (mat_high[...], mat_low[...])
    left = 0
    for sig in sigs:
        for inner in range(0, sig.shape[1], WIDE):
            here = slice(left, left + WIDE)
            parts = halves(jnp.concatenate([sig[:, inner : inner + WIDE], cur[:, here], prev[:, here]], axis=1))
            q_next[:, here] = dot3(parts, mats, ((1,), (0,)))
            left += WIDE


def call_last(sums, b_prev, cur, prev, sigs, nblock, count, tile):
    rows, cols = cur.shape
    spec = pl.BlockSpec((tile, cols), lambda g: (g, 0))
    small = pl.BlockSpec((nblock, nblock), lambda g: (0, 0))
    return pl.pallas_call(
        functools.partial(last_kernel, nblock, count, len(sigs)),
        grid=(rows // tile,),
        in_specs=[pl.BlockSpec(sums.shape, lambda g: (0, 0)), small, spec, spec]
        + [pl.BlockSpec((tile, s.shape[1]), lambda g: (g, 0)) for s in sigs],
        out_specs=[spec, small, small],
        out_shape=[
            jax.ShapeDtypeStruct((rows, cols), F32),
            jax.ShapeDtypeStruct((nblock, nblock), F32),
            jax.ShapeDtypeStruct((nblock, nblock), F32),
        ],
        scratch_shapes=[pltpu.VMEM((3 * WIDE, WIDE), BF)] * 2,
        compiler_params=pltpu.CompilerParams(vmem_limit_bytes=32 * MIB),
        cost_estimate=pl.CostEstimate(flops=18 * rows * cols * WIDE, bytes_accessed=16 * rows * cols, transcendentals=0),
        name="last",
    )(sums, b_prev, cur, prev, *sigs)


def total_over(value, axis, size):
    step = 1
    while step < size:
        value = value + lax.ppermute(value, axis, [(i, i ^ step) for i in range(size)])
        step *= 2
    return value


def ring_body(n_occ, n_vir, w_cycle, q_cur, q_prev, b_prev, e_vir, e_occ):
    v_loc, o_loc, columns = q_cur.shape
    nblock = b_prev.shape[0]
    j_count = columns // nblock
    n_z = n_occ // 2
    occ, vir = lax.axis_index("occ"), lax.axis_index("vir")
    z, y = occ // 2, occ % 2
    ring = [(o, (o + 2) % n_occ) for o in range(n_occ)]
    side = [(o, o ^ 1) for o in range(n_occ)]
    core = [(v, v ^ 1) for v in range(n_vir)]
    chip = [(v, v ^ 2) for v in range(n_vir)]
    groups = [jnp.stack([vir ^ 3, vir ^ 1]), jnp.stack([vir ^ 2, vir])]
    rows = v_loc * o_loc
    cur = q_cur.reshape(rows, columns)
    prev = q_prev.reshape(rows, columns)
    chunks = [(0, columns - WIDE), (columns - WIDE, columns)]

    own = [jnp.transpose(q_cur[:, :, a:b].astype(BF), (1, 0, 2)) for a, b in chunks]
    base = call_old(cur, prev, nblock, rows // 4)
    my_occ = lax.dynamic_slice_in_dim(e_occ, occ * o_loc, o_loc, 0)
    row_gap = jnp.broadcast_to((e_vir[:, None] - my_occ[None, :]).reshape(rows, 1), (rows, LANES))
    col_gap = jnp.broadcast_to(e_occ[:j_count, None], (j_count, nblock)).reshape(1, columns)

    turned = {}
    sigs = []
    for c, (a, b) in enumerate(chunks):
        line = [own[c]]
        beside = [lax.ppermute(own[c], "occ", side)]
        for t in range(1, n_z):
            line.append(lax.ppermute(line[-1], "occ", ring))
            if c > 0 and t == 1:
                beside.append(lax.ppermute(beside[0], "occ", ring))
            else:
                beside.append(lax.ppermute(line[-1], "occ", side))
        accs = [None, None]
        for t in range(n_z):
            at = (z + n_z - t) % n_z * 2
            for h in range(2):
                if c == 0:
                    pos = jnp.concatenate([groups[h], jnp.stack([at + y, at + 1 - y])]).astype(jnp.int32)
                    accs[h], turned[t, h] = call_first(w_cycle, line[t], beside[t], accs[h], pos, v_loc, v_loc // 2)
                else:
                    accs[h] = call_later(turned[t, h], line[t], beside[t], accs[h], rows // 2)
        came = lax.ppermute(accs[0], "vir", core)
        away = (accs[1][:rows] + came[:rows]).astype(BF)
        keep = accs[1][rows:] + came[rows:]
        other = lax.ppermute(away, "vir", chip)
        sig, base = call_sigma(keep, 0, other, cur, prev, row_gap, col_gap, base, nblock, a, rows // 4)
        sigs.append(sig)
    sums = total_over(total_over(base, "vir", n_vir), "occ", n_occ)
    count = float(rows * j_count * n_occ * n_vir)
    q_next, alpha, b_next = call_last(sums, b_prev, cur, prev, sigs, nblock, count, rows // 4)
    return q_next.reshape(v_loc, o_loc, columns), alpha, b_next


def plain_body(n_occ, n_vir, w_cycle, q_cur, q_prev, b_prev, e_vir, e_occ):
    v_loc, o_loc, columns = q_cur.shape
    nblock = b_prev.shape[0]
    j_count = columns // nblock
    count = v_loc * n_vir * o_loc * n_occ * j_count
    inner = lambda l, r: jnp.einsum("aijn,aijm->nm", l, r, precision=HIGH) / count
    apply = lambda l, m: jnp.einsum("aijn,nm->aijm", l, m, precision=HIGH)
    mul = lambda l, r: jnp.matmul(l, r, precision=HIGH)
    gathered = lax.all_gather(q_cur.astype(BF), "occ", axis=1, tiled=True)
    cycle_term = lax.psum_scatter(
        jnp.einsum("aikb,bkc->aic", w_cycle, gathered, preferred_element_type=F32), "vir", scatter_dimension=0, tiled=True
    )
    my_occ = lax.dynamic_slice_in_dim(e_occ, lax.axis_index("occ") * o_loc, o_loc, 0)
    gap = e_vir[:, None, None] - my_occ[None, :, None] - e_occ[None, None, :j_count]
    shape = (v_loc, o_loc, j_count, nblock)
    cur, prev = q_cur.reshape(shape), q_prev.reshape(shape)
    sigma = cycle_term.reshape(shape) + gap[:, :, :, None] * cur
    upper_t = jnp.triu(b_prev).T
    ss, cs, ps, cc, cp, pp = lax.psum(
        (inner(sigma, sigma), inner(cur, sigma), inner(prev, sigma), inner(cur, cur), inner(cur, prev), inner(prev, prev)),
        ("occ", "vir"),
    )
    residual = sigma - apply(cur, cs) - apply(prev, upper_t)
    gram = ss - mul(cs.T, cs) - mul(cs.T, cs) - mul(ps.T, upper_t) - mul(upper_t.T, ps)
    gram = gram + mul(cs.T, mul(cc, cs) + mul(cp, upper_t)) + mul(upper_t.T, mul(cp.T, cs) + mul(pp, upper_t))
    lower = jnp.linalg.cholesky(gram)
    inverse = jax.scipy.linalg.solve_triangular(lower, jnp.eye(nblock, dtype=F32), lower=True).T
    return apply(residual, inverse).reshape(v_loc, o_loc, columns), cs, lower.T


def solution(mesh):
    n_occ, n_vir = mesh.shape["occ"], mesh.shape["vir"]

    def body(w_cycle, q_cur, q_prev, b_prev, e_vir, e_occ):
        v_loc, o_loc, columns = q_cur.shape
        nblock = b_prev.shape[0]
        fits = (
            n_occ >= 4
            and n_occ & (n_occ - 1) == 0
            and n_vir == 4
            and o_loc == 8
            and v_loc % 32 == 0
            and v_loc % LANES == 0
            and columns % WIDE == 0
            and (columns - WIDE) % WIDE == 0
            and (columns - WIDE) > 0
            and 3 * nblock <= LANES
            and LANES % nblock == 0
            and nblock % 8 == 0
        )
        run = ring_body if fits else plain_body
        return run(n_occ, n_vir, w_cycle, q_cur, q_prev, b_prev, e_vir, e_occ)

    in_specs = (
        P(None, "occ", None, "vir"),
        P("vir", "occ", None),
        P("vir", "occ", None),
        P(),
        P("vir"),
        P(),
    )
    out_specs = (P("vir", "occ", None), P(), P())
    return jax.shard_map(body, mesh=mesh, in_specs=in_specs, out_specs=out_specs, check_vma=False)
```

```python
import functools

import jax
import jax.numpy as jnp
from jax import lax
from jax.experimental import pallas as pl
from jax.experimental.pallas import tpu as pltpu
from jax.sharding import PartitionSpec as P


BF = jnp.bfloat16
F32 = jnp.float32
HIGH = lax.Precision.HIGHEST
WIDE = 256
LANES = 128
MIB = 1 << 20


def dot(left, right, dims=((1,), (0,)), precision=None):
    return lax.dot_general(left, right, (dims, ((), ())), precision=precision, preferred_element_type=F32)


def halves(value):
    high = value.astype(BF)
    return high, (value - high.astype(F32)).astype(BF)


def dot3(left, right, dims):
    (lh, ll), (rh, rl) = left, right
    return dot(lh, rh, dims) + dot(lh, rl, dims) + dot(ll, rh, dims)


def cycle_first(add, pos, w0, w1, q0, q1, *rest):
    acc = rest[0] if add else None
    out, turned = rest[-2:]
    rows = w0.shape[0] * w0.shape[1]
    depth = w0.shape[2]
    total = acc[...] if add else None
    for place, (w, q) in enumerate(((w0, q0), (w1, q1))):
        by_k = jnp.swapaxes(w[...].astype(F32), 1, 2)
        parts = [by_k[:, k].reshape(rows, w.shape[3]).astype(BF) for k in range(depth)]
        for k in range(depth):
            turned[place * depth + k] = parts[k]
        term = dot(jnp.concatenate(parts, axis=1), q[...].reshape(depth * q.shape[1], q.shape[2]))
        total = term if total is None else total + term
    out[...] = total


def cycle_later(add, turned, q0, q1, *rest):
    acc = rest[0] if add else None
    out = rest[-1]
    depth = q0.shape[0]
    total = acc[...] if add else None
    for place, q in enumerate((q0, q1)):
        lhs = jnp.concatenate([turned[place * depth + k] for k in range(depth)], axis=1)
        term = dot(lhs, q[...].reshape(depth * q.shape[1], q.shape[2]))
        total = term if total is None else total + term
    out[...] = total


def call_first(w, q0, q1, acc, pos, v_loc, tile):
    _, o_loc, _, b_loc = w.shape
    depth, _, cols = q0.shape
    per = v_loc // tile
    steps = 2 * per
    rows = tile * o_loc
    full = 2 * v_loc * o_loc
    wspec = lambda s: pl.BlockSpec(
        (tile, o_loc, depth, b_loc), lambda g, p: (p[g // per] * per + g % per, 0, p[2 + s], 0)
    )
    qspec = pl.BlockSpec((depth, b_loc, cols), lambda g, p: (0, 0, 0))
    aspec = pl.BlockSpec((rows, cols), lambda g, p: (g, 0))
    add = acc is not None
    return pl.pallas_call(
        functools.partial(cycle_first, add),
        grid_spec=pltpu.PrefetchScalarGridSpec(
            num_scalar_prefetch=1,
            grid=(steps,),
            in_specs=[wspec(0), wspec(1), qspec, qspec] + ([aspec] if add else []),
            out_specs=[aspec, pl.BlockSpec((2 * depth, rows, b_loc), lambda g, p: (0, g, 0))],
        ),
        out_shape=[
            jax.ShapeDtypeStruct((full, cols), F32),
            jax.ShapeDtypeStruct((2 * depth, full, b_loc), BF),
        ],
        input_output_aliases={5: 0} if add else {},
        compiler_params=pltpu.CompilerParams(vmem_limit_bytes=44 * MIB),
        cost_estimate=pl.CostEstimate(
            flops=4 * full * depth * b_loc * cols, bytes_accessed=full * (8 * depth * b_loc + 8 * cols), transcendentals=0
        ),
        name="cycle_first",
    )(pos, w, w, q0, q1, *([acc] if add else []))


def call_later(turned, q0, q1, acc, rows):
    depth, b_loc, cols = q0.shape
    full = turned.shape[1]
    aspec = pl.BlockSpec((rows, cols), lambda g: (g, 0))
    qspec = pl.BlockSpec((depth, b_loc, cols), lambda g: (0, 0, 0))
    add = acc is not None
    return pl.pallas_call(
        functools.partial(cycle_later, add),
        grid=(full // rows,),
        in_specs=[pl.BlockSpec((2 * depth, rows, b_loc), lambda g: (0, g, 0)), qspec, qspec] + ([aspec] if add else []),
        out_specs=aspec,
        out_shape=jax.ShapeDtypeStruct((full, cols), F32),
        input_output_aliases={3: 0} if add else {},
        compiler_params=pltpu.CompilerParams(vmem_limit_bytes=44 * MIB),
        cost_estimate=pl.CostEstimate(
            flops=4 * full * depth * b_loc * cols, bytes_accessed=full * (4 * depth * b_loc + 8 * cols), transcendentals=0
        ),
        name="cycle_later",
    )(turned, q0, q1, *([acc] if add else []))


def fold(block, nblock):
    height, width = block.shape
    row = lax.broadcasted_iota(jnp.int32, (WIDE, width), 0) // nblock
    col = lax.broadcasted_iota(jnp.int32, (WIDE, width), 1) // nblock
    sums = []
    for top in range(0, height, WIDE):
        kept = jnp.where(row == col, block[top : top + WIDE], 0.0)
        sums.append(kept.reshape(WIDE // nblock, nblock, width).sum(0))
    total = jnp.concatenate(sums, axis=0)
    lanes = total[:, :LANES]
    for left in range(LANES, width, LANES):
        lanes = lanes + total[:, left : left + LANES]
    shift = LANES // 2
    while shift >= nblock:
        lanes = lanes + pltpu.roll(lanes, shift, 1)
        shift //= 2
    return lanes


def old_kernel(nblock, cur, prev, out, total):
    step = pl.program_id(0)

    @pl.when(step == 0)
    def _():
        total[...] = jnp.zeros_like(total)

    for left in range(0, cur.shape[1], WIDE):
        both = jnp.concatenate([cur[:, left : left + WIDE], prev[:, left : left + WIDE]], axis=1)
        parts = halves(both)
        total[...] += dot3(parts, parts, ((0,), (0,)))

    @pl.when(step == pl.num_programs(0) - 1)
    def _():
        lane = lax.broadcasted_iota(jnp.int32, (2 * nblock, LANES), 1)
        mine = fold(total[:, :WIDE], nblock)
        other = fold(total[:, WIDE:], nblock)
        value = jnp.where((lane >= nblock) & (lane < 2 * nblock), mine, 0.0)
        value = jnp.where((lane >= 2 * nblock) & (lane < 3 * nblock), other, value)
        out[...] = jnp.concatenate([jnp.zeros((nblock, LANES), F32), value], axis=0)


def call_old(cur, prev, nblock, tile):
    rows, cols = cur.shape
    spec = pl.BlockSpec((tile, cols), lambda g: (g, 0))
    return pl.pallas_call(
        functools.partial(old_kernel, nblock),
        grid=(rows // tile,),
        in_specs=[spec, spec],
        out_specs=pl.BlockSpec((3 * nblock, LANES), lambda g: (0, 0)),
        out_shape=jax.ShapeDtypeStruct((3 * nblock, LANES), F32),
        scratch_shapes=[pltpu.VMEM((2 * WIDE, 2 * WIDE), F32)],
        compiler_params=pltpu.CompilerParams(vmem_limit_bytes=32 * MIB),
        cost_estimate=pl.CostEstimate(flops=12 * rows * cols * 2 * WIDE, bytes_accessed=8 * rows * cols, transcendentals=0),
        name="old_blocks",
    )(cur, prev)


def sigma_kernel(nblock, keep, came, cur, prev, row_gap, col_gap, base, sig, out, total):
    step = pl.program_id(0)

    @pl.when(step == 0)
    def _():
        total[...] = jnp.zeros_like(total)

    for left in range(0, cur.shape[1], WIDE):
        here = slice(left, left + WIDE)
        q = cur[:, here]
        gap = jnp.tile(row_gap[...], (1, WIDE // LANES)) - col_gap[:, here]
        value = keep[:, here] + came[:, here].astype(F32) + gap * q
        sig[:, here] = value
        vh, vl = halves(value)
        ch, cl = halves(q)
        ph, pw = halves(prev[:, here])
        highs = jnp.concatenate([vh, ch, ph], axis=1)
        lows = jnp.concatenate([vl, cl, pw], axis=1)
        total[...] += dot3((highs, lows), (vh, vl), ((0,), (0,)))

    @pl.when(step == pl.num_programs(0) - 1)
    def _():
        lane = lax.broadcasted_iota(jnp.int32, (3 * nblock, LANES), 1)
        out[...] = base[...] + jnp.where(lane < nblock, fold(total[...], nblock), 0.0)


def call_sigma(keep, keep_block, came, cur, prev, row_gap, col_gap, base, nblock, left, tile):
    rows = cur.shape[0]
    cols = came.shape[1]
    per = rows // tile
    spec = pl.BlockSpec((tile, cols), lambda g: (g, 0))
    at = left // cols
    qspec = pl.BlockSpec((tile, cols), lambda g: (g, at))
    whole = pl.BlockSpec((3 * nblock, LANES), lambda g: (0, 0))
    return pl.pallas_call(
        functools.partial(sigma_kernel, nblock),
        grid=(per,),
        in_specs=[
            pl.BlockSpec((tile, cols), lambda g: (keep_block * per + g, 0)),
            spec,
            qspec,
            qspec,
            pl.BlockSpec((tile, LANES), lambda g: (g, 0)),
            pl.BlockSpec((1, cols), lambda g: (0, at)),
            whole,
        ],
        out_specs=[spec, whole],
        out_shape=[jax.ShapeDtypeStruct((rows, cols), F32), jax.ShapeDtypeStruct((3 * nblock, LANES), F32)],
        scratch_shapes=[pltpu.VMEM((3 * WIDE, WIDE), F32)],
        compiler_params=pltpu.CompilerParams(vmem_limit_bytes=32 * MIB),
        cost_estimate=pl.CostEstimate(flops=18 * rows * cols * WIDE, bytes_accessed=18 * rows * cols, transcendentals=0),
        name="sigma",
    )(keep, came, cur, prev, row_gap, col_gap, base)


def last_kernel(nblock, count, n_sig, sums, b_prev, cur, prev, *rest):
    sigs, (q_next, alpha_out, b_next, mat_high, mat_low) = rest[:n_sig], rest[n_sig:]

    @pl.when(pl.program_id(0) == 0)
    def _():
        n = nblock
        k = sums[...] / count
        alpha = k[n : 2 * n, :n]
        row = lax.broadcasted_iota(jnp.int32, (n, n), 0)
        col = lax.broadcasted_iota(jnp.int32, (n, n), 1)
        upper = jnp.where(row <= col, b_prev[...], 0.0)
        upper_t = upper.T
        z = jnp.concatenate([-alpha, -upper_t], axis=0)
        k_rs = k[n : 3 * n, :n]
        k_rr = k[n : 3 * n, n : 3 * n]
        lead = ((0,), (0,))
        v = dot(k_rr, z, precision=HIGH)
        gram = (k[:n, :n] + dot(k_rs, z, lead, HIGH)) + dot(z, k_rs + v, lead, HIGH)
        lane = lax.broadcasted_iota(jnp.int32, (n, LANES), 1)
        line = lax.broadcasted_iota(jnp.int32, (n, LANES), 0)
        aug = jnp.concatenate([gram, jnp.zeros((n, LANES - n), F32)], axis=1)
        aug = aug + jnp.where(lane == line + n, 1.0, 0.0)
        for i in range(n):
            root = jnp.sqrt(aug[i : i + 1, i : i + 1])
            scaled = aug[i : i + 1, :] / root
            factor = aug[:, i : i + 1] / root
            aug = jnp.where(line == i, scaled, jnp.where(line > i, aug - factor * scaled, aug))
        alpha_out[...] = alpha
        b_next[...] = jnp.where(row <= col, aug[:, :n], 0.0)
        low_inv = aug[:, n : 2 * n]
        eye = jnp.where(row == col, 1.0, 0.0)
        mats = dot(jnp.concatenate([eye, z], axis=0), low_inv, ((1,), (1,)), HIGH)
        spread = jnp.where(
            lax.broadcasted_iota(jnp.int32, (n, WIDE), 1) % n == lax.broadcasted_iota(jnp.int32, (n, WIDE), 0), 1.0, 0.0
        )
        wide = dot(mats, spread, precision=HIGH)
        same = (
            lax.broadcasted_iota(jnp.int32, (WIDE, WIDE), 0) // n == lax.broadcasted_iota(jnp.int32, (WIDE, WIDE), 1) // n
        )
        for part in range(3):
            block = jnp.concatenate([wide[part * n : (part + 1) * n]] * (WIDE // n), axis=0)
            high, low = halves(jnp.where(same, block, 0.0))
            mat_high[part * WIDE : (part + 1) * WIDE] = high
            mat_low[part * WIDE : (part + 1) * WIDE] = low

    mats = (mat_high[...], mat_low[...])
    left = 0
    for sig in sigs:
        for inner in range(0, sig.shape[1], WIDE):
            here = slice(left, left + WIDE)
            parts = halves(jnp.concatenate([sig[:, inner : inner + WIDE], cur[:, here], prev[:, here]], axis=1))
            q_next[:, here] = dot3(parts, mats, ((1,), (0,)))
            left += WIDE


def call_last(sums, b_prev, cur, prev, sigs, nblock, count, tile):
    rows, cols = cur.shape
    spec = pl.BlockSpec((tile, cols), lambda g: (g, 0))
    small = pl.BlockSpec((nblock, nblock), lambda g: (0, 0))
    return pl.pallas_call(
        functools.partial(last_kernel, nblock, count, len(sigs)),
        grid=(rows // tile,),
        in_specs=[pl.BlockSpec(sums.shape, lambda g: (0, 0)), small, spec, spec]
        + [pl.BlockSpec((tile, s.shape[1]), lambda g: (g, 0)) for s in sigs],
        out_specs=[spec, small, small],
        out_shape=[
            jax.ShapeDtypeStruct((rows, cols), F32),
            jax.ShapeDtypeStruct((nblock, nblock), F32),
            jax.ShapeDtypeStruct((nblock, nblock), F32),
        ],
        scratch_shapes=[pltpu.VMEM((3 * WIDE, WIDE), BF)] * 2,
        compiler_params=pltpu.CompilerParams(vmem_limit_bytes=32 * MIB),
        cost_estimate=pl.CostEstimate(flops=18 * rows * cols * WIDE, bytes_accessed=16 * rows * cols, transcendentals=0),
        name="last",
    )(sums, b_prev, cur, prev, *sigs)


def total_over(value, axis, size):
    step = 1
    while step < size:
        value = value + lax.ppermute(value, axis, [(i, i ^ step) for i in range(size)])
        step *= 2
    return value


def ring_body(n_occ, n_vir, w_cycle, q_cur, q_prev, b_prev, e_vir, e_occ):
    v_loc, o_loc, columns = q_cur.shape
    nblock = b_prev.shape[0]
    j_count = columns // nblock
    n_z = n_occ // 2
    occ, vir = lax.axis_index("occ"), lax.axis_index("vir")
    z, y = occ // 2, occ % 2
    ring = [(o, (o + 2) % n_occ) for o in range(n_occ)]
    side = [(o, o ^ 1) for o in range(n_occ)]
    core = [(v, v ^ 1) for v in range(n_vir)]
    chip = [(v, v ^ 2) for v in range(n_vir)]
    groups = [jnp.stack([vir ^ 3, vir ^ 1]), jnp.stack([vir ^ 2, vir])]
    rows = v_loc * o_loc
    cur = q_cur.reshape(rows, columns)
    prev = q_prev.reshape(rows, columns)
    chunks = [(0, columns - WIDE), (columns - WIDE, columns)]

    own = [jnp.transpose(q_cur[:, :, a:b].astype(BF), (1, 0, 2)) for a, b in chunks]
    base = call_old(cur, prev, nblock, rows // 4)
    my_occ = lax.dynamic_slice_in_dim(e_occ, occ * o_loc, o_loc, 0)
    row_gap = jnp.broadcast_to((e_vir[:, None] - my_occ[None, :]).reshape(rows, 1), (rows, LANES))
    col_gap = jnp.broadcast_to(e_occ[:j_count, None], (j_count, nblock)).reshape(1, columns)

    turned = {}
    sigs = []
    for c, (a, b) in enumerate(chunks):
        line = [own[c]]
        beside = [lax.ppermute(own[c], "occ", side)]
        for t in range(1, n_z):
            line.append(lax.ppermute(line[-1], "occ", ring))
            if c > 0 and t == 1:
                beside.append(lax.ppermute(beside[0], "occ", ring))
            else:
                beside.append(lax.ppermute(line[-1], "occ", side))
        accs = [None, None]
        for t in range(n_z):
            at = (z + n_z - t) % n_z * 2
            for h in range(2):
                if c == 0:
                    pos = jnp.concatenate([groups[h], jnp.stack([at + y, at + 1 - y])]).astype(jnp.int32)
                    accs[h], turned[t, h] = call_first(w_cycle, line[t], beside[t], accs[h], pos, v_loc, v_loc // 2)
                else:
                    accs[h] = call_later(turned[t, h], line[t], beside[t], accs[h], rows)
        came = lax.ppermute(accs[0], "vir", core)
        away = (accs[1][:rows] + came[:rows]).astype(BF)
        keep = accs[1][rows:] + came[rows:]
        other = lax.ppermute(away, "vir", chip)
        sig, base = call_sigma(keep, 0, other, cur, prev, row_gap, col_gap, base, nblock, a, rows // 4)
        sigs.append(sig)
    sums = total_over(total_over(base, "vir", n_vir), "occ", n_occ)
    count = float(rows * j_count * n_occ * n_vir)
    q_next, alpha, b_next = call_last(sums, b_prev, cur, prev, sigs, nblock, count, rows // 4)
    return q_next.reshape(v_loc, o_loc, columns), alpha, b_next


def plain_body(n_occ, n_vir, w_cycle, q_cur, q_prev, b_prev, e_vir, e_occ):
    v_loc, o_loc, columns = q_cur.shape
    nblock = b_prev.shape[0]
    j_count = columns // nblock
    count = v_loc * n_vir * o_loc * n_occ * j_count
    inner = lambda l, r: jnp.einsum("aijn,aijm->nm", l, r, precision=HIGH) / count
    apply = lambda l, m: jnp.einsum("aijn,nm->aijm", l, m, precision=HIGH)
    mul = lambda l, r: jnp.matmul(l, r, precision=HIGH)
    gathered = lax.all_gather(q_cur.astype(BF), "occ", axis=1, tiled=True)
    cycle_term = lax.psum_scatter(
        jnp.einsum("aikb,bkc->aic", w_cycle, gathered, preferred_element_type=F32), "vir", scatter_dimension=0, tiled=True
    )
    my_occ = lax.dynamic_slice_in_dim(e_occ, lax.axis_index("occ") * o_loc, o_loc, 0)
    gap = e_vir[:, None, None] - my_occ[None, :, None] - e_occ[None, None, :j_count]
    shape = (v_loc, o_loc, j_count, nblock)
    cur, prev = q_cur.reshape(shape), q_prev.reshape(shape)
    sigma = cycle_term.reshape(shape) + gap[:, :, :, None] * cur
    upper_t = jnp.triu(b_prev).T
    ss, cs, ps, cc, cp, pp = lax.psum(
        (inner(sigma, sigma), inner(cur, sigma), inner(prev, sigma), inner(cur, cur), inner(cur, prev), inner(prev, prev)),
        ("occ", "vir"),
    )
    residual = sigma - apply(cur, cs) - apply(prev, upper_t)
    gram = ss - mul(cs.T, cs) - mul(cs.T, cs) - mul(ps.T, upper_t) - mul(upper_t.T, ps)
    gram = gram + mul(cs.T, mul(cc, cs) + mul(cp, upper_t)) + mul(upper_t.T, mul(cp.T, cs) + mul(pp, upper_t))
    lower = jnp.linalg.cholesky(gram)
    inverse = jax.scipy.linalg.solve_triangular(lower, jnp.eye(nblock, dtype=F32), lower=True).T
    return apply(residual, inverse).reshape(v_loc, o_loc, columns), cs, lower.T


def solution(mesh):
    n_occ, n_vir = mesh.shape["occ"], mesh.shape["vir"]

    def body(w_cycle, q_cur, q_prev, b_prev, e_vir, e_occ):
        v_loc, o_loc, columns = q_cur.shape
        nblock = b_prev.shape[0]
        fits = (
            n_occ >= 8
            and n_occ & (n_occ - 1) == 0
            and n_vir == 4
            and o_loc == 8
            and v_loc % 32 == 0
            and v_loc % LANES == 0
            and columns % WIDE == 0
            and (columns - WIDE) % WIDE == 0
            and (columns - WIDE) > 0
            and 3 * nblock <= LANES
            and LANES % nblock == 0
            and nblock % 8 == 0
        )
        if not fits:
            return plain_body(n_occ, n_vir, w_cycle, q_cur, q_prev, b_prev, e_vir, e_occ)
        return ring_body(n_occ, n_vir, w_cycle, q_cur, q_prev, b_prev, e_vir, e_occ)

    in_specs = (
        P(None, "occ", None, "vir"),
        P("vir", "occ", None),
        P("vir", "occ", None),
        P(),
        P("vir"),
        P(),
    )
    out_specs = (P("vir", "occ", None), P(), P())
    return jax.shard_map(body, mesh=mesh, in_specs=in_specs, out_specs=out_specs, check_vma=False)
```
